32 devices in a mesh: space: 8 (over z, y), scen: 4 (over x, core).
Axes of the slice: x: 2, y: 2, z: 4, core: 2. Of those that a mesh axis runs over, the one named last changes fastest.
Arguments:
- start_fraction: bfloat16 [16, 24, 16384], P('scen', None, 'space'), may hold values from 0 to 1
- ore_value: bfloat16 [16, 24, 16384], P('scen', None, 'space'), may hold values from -6 to 6
- dual_price: float32 [16, 24, 16384], P('scen', None, 'space'), may hold values from -3 to 3
- patterns: bfloat16 [3, 512, 512], replicated, may hold values from -0.15625 to 0.15625
- cone_list: int32 [32, 3], P('space'), may hold values from 0 to 31, as said below
- node_list: int32 [2, 16], replicated, may hold values from 0 to 15, as said below
- probability: float32 [16], replicated, may hold values from 0.5 to 2
Outputs:
- fraction: float32 [16, 24, 16384], P('scen', None, 'space')
- dual_out: float32 [16, 24, 16384], P('scen', None, 'space')
The draws below stay inside these ranges and needn't reach their ends.
Inputs may be any that keep to these rules, and one draw needn't show every extreme that they name: `cone_list`: row i holds i, then tile i - 1 and tile i + 1 in an order drawn per tile; where a neighbour lies outside the slab the tile itself stands in its place. `node_list`: row 0 holds second-section nodes below 4, row 1 third-section nodes; every node holds a scenario, and scenarios that share a third-section node share their second-section node.
All inputs are finite; a program needn't handle non-finite values.
Results may differ from the reference program's by a relative error of at most 0.00079.
Values may be sent and summed in bfloat16 or wider, within the bound.
No kernel may reach another device: no remote copies, remote signals or barrier semaphores. Data moves between devices by JAX's collectives and lax.ppermute only.
A program may use at most 64 MiB of HBM per device.

```python
import math
import jax
import jax.numpy as jnp
from jax import lax

TILE = 512
PERIODS = 24
SECTIONS = 4
NODES1 = 4
NODES2 = 16
ITERS = 2
PG_STEPS = 2
SCEN = 16
TILES = 32
BLOCKS = 16384


def draw_cone_list(key, part):
    tile_ids = jnp.arange(TILES, dtype=jnp.int32)
    flips = jax.random.randint(jax.random.fold_in(key, 11), (TILES,), 0, 2)
    left_tile = jnp.where(tile_ids == 0, tile_ids, tile_ids - 1)
    right_tile = jnp.where(tile_ids == TILES - 1, tile_ids, tile_ids + 1)
    first_slot = jnp.where(flips == 1, left_tile, right_tile)
    second_slot = jnp.where(flips == 1, right_tile, left_tile)
    return jnp.stack([tile_ids, first_slot, second_slot], axis=1).astype(jnp.int32)


def draw_node_list(key, part):
    order = jax.random.permutation(jax.random.fold_in(key, 21), SCEN).astype(jnp.int32)
    filler = jax.random.randint(jax.random.fold_in(key, 22), (SCEN,), 0, NODES2)
    second_nodes = jnp.where(order < NODES2, order, filler).astype(jnp.int32)
    parents = jax.random.permutation(jax.random.fold_in(key, 23), NODES1).astype(jnp.int32)
    parent_of = jnp.take(parents, jnp.arange(NODES2, dtype=jnp.int32) % NODES1)
    first_nodes = jnp.take(parent_of, second_nodes).astype(jnp.int32)
    return jnp.stack([first_nodes, second_nodes], axis=0).astype(jnp.int32)


def levels(stream_key, extent, cuts, least, top_value):
    loudness, own = 1.0, jax.random.fold_in(stream_key, 6)
    for axis_at, parts in cuts:
        steps = jnp.exp(jax.random.uniform(jax.random.fold_in(own, axis_at), (parts,), jnp.float32, least / len(cuts), top_value / len(cuts)))
        loudness = loudness * jnp.repeat(steps, extent[axis_at] // parts).reshape([-1 if axis == axis_at else 1 for axis in range(len(extent))])
    return loudness


def scatter_about(own_key, extent, deviation, limit, shards=(), kind=jnp.bfloat16):
    level = levels(own_key, extent, shards, -0.22, 0.18) if shards else 1.0
    drawn = jax.random.normal(own_key, extent, jnp.float32) * deviation * level
    return jnp.minimum(jnp.maximum(drawn, -limit), limit).astype(kind)


def setup_inputs(seed: int = 0) -> dict:
    key_list = jax.random.split(jax.random.key(seed), 8)
    start_fraction = jnp.clip(1.0 * jax.random.uniform(key_list[0], (SCEN, PERIODS, BLOCKS), jnp.float32) ** levels(key_list[0], (SCEN, PERIODS, BLOCKS), ((0, 4), (2, 8)), -0.2, 0.2), 0.0, 1.0).astype(jnp.bfloat16)
    ore_value = scatter_about(key_list[1], (SCEN, PERIODS, BLOCKS), 1.0, 6.0, ((0, 4), (2, 8)))
    dual_price = scatter_about(key_list[2], (SCEN, PERIODS, BLOCKS), 0.5, 3.0, ((0, 4), (2, 8)), jnp.float32)
    patterns = scatter_about(key_list[3], (3, TILE, TILE), (3 * TILE) ** -0.5, 0.15625)
    cone_list = draw_cone_list(jax.random.fold_in(key_list[7], 71), 0)
    node_list = draw_node_list(jax.random.fold_in(key_list[7], 71), 0)
    probability = jnp.clip(jnp.exp(jax.random.uniform(key_list[6], (SCEN,), jnp.float32, math.log(0.5), math.log(2.0))), 0.5, 2.0)
    return dict(start_fraction=start_fraction, ore_value=ore_value, dual_price=dual_price, patterns=patterns, cone_list=cone_list, node_list=node_list, probability=probability)


def node_weights(nodes, weights_in, count):
    return (nodes[:, None] == jnp.arange(count)[None, :]).astype(jnp.float32) * weights_in[:, None]


def upper_center(middle, node_list, probability, quarter):
    width_blocks = middle.shape[2]
    scen_count = middle.shape[0]
    root_sum = jnp.tensordot(probability, middle[:, :quarter], axes=1, precision=lax.Precision.HIGHEST)
    root_mean = root_sum / jnp.sum(probability)
    weight_one = node_weights(node_list[0], probability, NODES1)
    weight_two = node_weights(node_list[1], probability, NODES2)
    first_sum = jnp.tensordot(weight_one, middle[:, quarter:2 * quarter], axes=((0,), (0,)), precision=lax.Precision.HIGHEST)
    second_sum = jnp.tensordot(weight_two, middle[:, 2 * quarter:3 * quarter], axes=((0,), (0,)), precision=lax.Precision.HIGHEST)
    first_mean = first_sum / jnp.sum(weight_one, axis=0)[:, None, None]
    second_mean = second_sum / jnp.sum(weight_two, axis=0)[:, None, None]
    root_part = jnp.broadcast_to(root_mean[None], (scen_count, quarter, width_blocks))
    first_part = jnp.take(first_mean, node_list[0], axis=0)
    second_part = jnp.take(second_mean, node_list[1], axis=0)
    return jnp.concatenate([root_part, first_part, second_part], axis=1)


def tree_center(fraction, node_list, probability):
    quarter = fraction.shape[1] // SECTIONS
    upper = upper_center(fraction[:, :(SECTIONS - 1) * quarter], node_list, probability, quarter)
    return jnp.concatenate([upper, fraction[:, (SECTIONS - 1) * quarter:]], axis=1)


def descend(fraction, ore_value, dual_now, center, cone_list, patterns):
    rounded = fraction.astype(jnp.bfloat16)
    full_shape = fraction.shape
    tile_view = rounded.reshape(full_shape[0], full_shape[1], full_shape[2] // TILE, TILE)
    accumulated = jnp.zeros((fraction.size // TILE, TILE), jnp.float32)
    for cone_slot in range(3):
        picked = jnp.take(tile_view, cone_list[:, cone_slot], axis=2).reshape(-1, TILE)
        accumulated = accumulated + jnp.dot(picked, patterns[cone_slot], preferred_element_type=jnp.float32)
    cone_mix = accumulated.reshape(full_shape)
    gradient = -ore_value.astype(jnp.float32) + dual_now + 1.0 * (fraction - center) + 1.0 * (fraction - cone_mix)
    return jnp.clip(fraction - 0.4 * gradient, 0.0, 1.0)


def reference(start_fraction, ore_value, dual_price, patterns, cone_list, node_list, probability):
    fraction = start_fraction.astype(jnp.float32)
    dual_now = dual_price
    center = tree_center(fraction, node_list, probability)
    for ph_round in range(ITERS):
        for inner_step in range(PG_STEPS):
            fraction = descend(fraction, ore_value, dual_now, center, cone_list, patterns)
        center = tree_center(fraction, node_list, probability)
        dual_now = dual_now + 1.0 * (fraction - center)
    return fraction, dual_now
```

```python
import functools
import jax
import jax.numpy as jnp
from jax import lax
from jax.experimental import pallas as pl
from jax.experimental.pallas import tpu as pltpu
from jax.sharding import PartitionSpec as P

TILE = 512
SECTIONS = 4
NODES1 = 4
NODES2 = 16
ITERS = 2
PG_STEPS = 2
SUB = 8
AXES = ("space", "scen")
CHAINS = ((0, 16), (16, 24))

f32, bf16 = jnp.float32, jnp.bfloat16
VMEM = pl.BlockSpec(memory_space=pltpu.VMEM)
SMEM = pl.BlockSpec(memory_space=pltpu.SMEM)
CORE, EDGE, INNER, SLOT_IN, SLOT_OUT, END, SLOT_EDGE, SLOT_OTHER, NODES = range(9)


def call(kernel, name, control, arrays, out):
    shapes = [jax.ShapeDtypeStruct(s, d) for s, d in out]
    return pl.pallas_call(
        kernel,
        out_shape=shapes,
        in_specs=[SMEM] * len(control) + [VMEM] * len(arrays),
        out_specs=[VMEM] * len(shapes),
        name=name,
        compiler_params=pltpu.CompilerParams(vmem_limit_bytes=48 << 20),
    )(*control, *arrays)


def lanes(tile):
    return pl.ds(pl.multiple_of(tile * TILE, TILE), TILE)


class Plan:
    def __init__(self, mesh, fraction, cone_list, node_list):
        self.spaces, self.scens = mesh.shape["space"], mesh.shape["scen"]
        self.rank, self.periods, width = fraction.shape
        self.tiles = cone_list.shape[0]
        self.quarter = self.periods // SECTIONS
        self.local = 2 * self.rank
        self.second = node_list.shape[1] > NODES2
        self.blocks = 1 + NODES1 + (NODES2 if self.second else 0)
        self.reach = (3 if self.second else 2) * self.quarter
        self.chains = tuple((lo, hi) for lo, hi in CHAINS)

    def averaged(self, chain):
        return chain[0] < self.reach

    def section(self, low, which):
        first, last = which * self.quarter, (which + 1) * self.quarter
        if low + SUB <= first or low >= last:
            return None
        if first <= low and low + SUB <= last:
            return True
        period = low + lax.broadcasted_iota(jnp.int32, (SUB, TILE), 0)
        return (period >= first) & (period < last)


def put(mask, new, old):
    return old if mask is None else new if mask is True else jnp.where(mask, new, old)


def partial_means(plan, chain, control, weights, edge, inner, sums):
    lo, hi = chain
    size = hi - lo
    for side, source in enumerate((edge, inner)):
        for block in range(plan.blocks):
            which = 0 if block == 0 else 1 if block <= NODES1 else 2
            total = jnp.zeros((SUB, TILE), f32)
            for low in range(lo, hi, SUB):
                mask = plan.section(low, which)
                if mask is None:
                    continue
                part = jnp.zeros((SUB, TILE), f32)
                for j in range(plan.local):
                    weight = weights[which * plan.local + j]
                    if which:
                        node = control[NODES + (which - 1) * plan.local + j]
                        first = 1 if which == 1 else 1 + NODES1
                        weight = jnp.where(node == block - first, weight, 0.0)
                    row = j * size + low - lo
                    part = part + weight * source[row : row + SUB, :]
                total = total + put(mask, part, jnp.zeros_like(part))
            sums[block, :, side * TILE : (side + 1) * TILE] = total


def center_rows(plan, low, side, nodes, means, value):
    span = slice(side * TILE, (side + 1) * TILE)
    value = put(plan.section(low, 0), means(0, span), value) if plan.section(low, 0) is not None else value
    mask = plan.section(low, 1)
    if mask is not None:
        value = put(mask, means(1 + nodes(0), span), value)
    mask = plan.section(low, 2)
    if plan.second and mask is not None:
        value = put(mask, means(1 + NODES1 + nodes(1), span), value)
    return value


def send_fraction(plan, control, start, out):
    other = 1 - control[CORE]
    edge, inner = other * (plan.tiles - 1), 1 + other * (plan.tiles - 3)
    out[0] = start[:, :, lanes(edge)]
    out[1] = start[:, :, lanes(inner)]


def send_drive(plan, control, ore, dual, out):
    other = 1 - control[CORE]
    for k, tile in enumerate((other * (plan.tiles - 1), 1 + other * (plan.tiles - 3))):
        out[k] = ore[:, :, lanes(tile)].astype(f32) - dual[:, :, lanes(tile)]


def assemble(plan, control, own, came, out):
    core = control[CORE]
    for (lo, hi), pair in zip(plan.chains, out):
        size = hi - lo
        for k, ref in enumerate(pair):
            for r in range(plan.rank):
                mine = pl.multiple_of((core * plan.rank + r) * size, SUB)
                theirs = pl.multiple_of(((1 - core) * plan.rank + r) * size, SUB)
                ref[pl.ds(mine, size), :] = own(k, r, lo, hi).astype(f32)
                ref[pl.ds(theirs, size), :] = came[k, r, lo:hi, :].astype(f32)


def start_kernel(plan, control, weights, start, came, *outs):
    n = len(plan.chains)
    state = [outs[2 * c : 2 * c + 2] for c in range(n)]
    sends = [outs[2 * n + 2 * c : 2 * n + 2 * c + 2] for c in range(n)]
    tiles = (control[EDGE], control[INNER])
    assemble(plan, control, lambda k, r, lo, hi: start[r, lo:hi, lanes(tiles[k])], came, state)
    for pair, send in zip(state, sends):
        for ref, out in zip(pair, send):
            out[...] = ref[...].astype(bf16)
    at = 4 * n
    for c, chain in enumerate(plan.chains):
        if plan.averaged(chain):
            partial_means(plan, chain, control, weights, *state[c], outs[at])
            at += 1


def drive_kernel(plan, control, ore, dual, came, *outs):
    tiles = (control[EDGE], control[INNER])

    def own(k, r, lo, hi):
        return ore[r, lo:hi, lanes(tiles[k])].astype(f32) - dual[r, lo:hi, lanes(tiles[k])]

    assemble(plan, control, own, came, [outs[2 * c : 2 * c + 2] for c in range(len(plan.chains))])


def inside(plan, chain, first, last_round, final, control, edge, inner, halo, drive_e, drive_n, patterns, *rest):
    lo, hi = chain
    size = hi - lo
    averaged = plan.averaged(chain)
    rest = list(rest)
    pull_e, pull_n = drive_e, drive_n
    if first:
        means_refs = (rest.pop(0), rest.pop(0)) if averaged else None
    base_e, next_n, send_n = rest[:3]
    rest = rest[3:]
    if first:
        pull_e, pull_n = rest[:2]
        rest = rest[2:]
        moved = rest[:2] if last_round and averaged else None
        if averaged:
            means = lambda block, span: means_refs[0][block, :, span] + means_refs[1][block, :, span]
        for side, (value, drive, pull) in enumerate(((edge, drive_e, pull_e), (inner, drive_n, pull_n))):
            for j in range(plan.local):
                for low in range(lo, hi, SUB):
                    rows = slice(j * size + low - lo, j * size + low - lo + SUB)
                    now = value[rows, :]
                    mean = now
                    if averaged:
                        nodes = lambda which: control[NODES + which * plan.local + j]
                        mean = center_rows(plan, low, side, nodes, means, now)
                    if last_round:
                        gap = now - mean
                        if averaged:
                            moved[side][rows, :] = gap
                        pull[rows, :] = drive[rows, :] - gap + mean
                    else:
                        pull[rows, :] = drive[rows, :] + mean
    round_e, round_n = edge[...].astype(bf16), inner[...].astype(bf16)
    dot = functools.partial(jnp.dot, preferred_element_type=f32)
    cone = dot(round_e, patterns[0]) + dot(round_n, patterns[control[SLOT_IN]])
    value = edge[...]
    base_e[...] = value - 0.4 * ((value - cone) + value - pull_e[...])
    cone = dot(round_n, patterns[0]) + dot(round_e, patterns[control[SLOT_EDGE]]) + dot(halo[...], patterns[control[SLOT_OTHER]])
    value = inner[...]
    value = jnp.clip(value - 0.4 * ((value - cone) + value - pull_n[...]), 0.0, 1.0)
    next_n[...] = value
    send_n[...] = value.astype(bf16)
    if final:
        count = plan.rank * size
        rest[0][...] = next_n[pl.ds(pl.multiple_of((1 - control[CORE]) * count, SUB), count), :]


def outside(plan, chain, means, final, control, weights, base, halo, round_e, patterns, *rest):
    rest = list(rest)
    inner = rest.pop(0) if means else None
    next_e, send_e = rest[:2]
    lhs = jnp.where(control[END] == 1, round_e[...].astype(f32), halo[...].astype(f32)).astype(bf16)
    cone = jnp.dot(lhs, patterns[control[SLOT_OUT]], preferred_element_type=f32)
    value = jnp.clip(base[...] + 0.4 * cone, 0.0, 1.0)
    next_e[...] = value
    send_e[...] = value.astype(bf16)
    rest = rest[2:]
    if means:
        partial_means(plan, chain, control, weights, next_e, inner, rest.pop(0))
    if final:
        count = plan.rank * (chain[1] - chain[0])
        rest[0][...] = next_e[pl.ds(pl.multiple_of((1 - control[CORE]) * count, SUB), count), :]


def finish_kernel(plan, control, *refs):
    refs = list(refs)
    dual = refs.pop(0)
    mean_refs = [(refs.pop(0), refs.pop(0)), (refs.pop(0), refs.pop(0))]
    fraction, dual_out = refs[-2:]
    core = control[CORE]
    tiles = ((control[EDGE], control[INNER]), ((1 - core) * (plan.tiles - 1), 1 + (1 - core) * (plan.tiles - 3)))
    at = 0
    for chain in plan.chains:
        lo, hi = chain
        size = hi - lo
        held = refs[at : at + 2]
        came = refs[at + 2 : at + 4]
        at += 4
        averaged = plan.averaged(chain)
        if averaged:
            moved, moved_came = refs[at : at + 2], refs[at + 2 : at + 4]
            at += 4
        for part in range(2):
            pair = mean_refs[part]
            means = lambda block, span: pair[0][block, :, span] + pair[1][block, :, span]
            for side in range(2):
                where = lanes(tiles[part][side])
                for r in range(plan.rank):
                    for low in range(lo, hi, SUB):
                        if part == 0:
                            row = pl.multiple_of((core * plan.rank + r) * size + low - lo, SUB)
                            now = held[side][pl.ds(row, SUB), :]
                        else:
                            row = r * size + low - lo
                            now = came[side][row : row + SUB, :]
                        out = (r, slice(low, low + SUB), where)
                        fraction[out] = now
                        price = dual[out]
                        if averaged and low < plan.reach:
                            nodes = lambda which: control[NODES + which * plan.local + core * plan.rank + r]
                            mean = center_rows(plan, low, side, nodes, means, now)
                            gap = moved[side][pl.ds(row, SUB), :] if part == 0 else moved_came[side][row : row + SUB, :]
                            price = (price + gap) + (now - mean)
                        dual_out[out] = price


def partners(plan):
    pairs = []
    for i in range(plan.spaces):
        for s in range(plan.scens):
            to = i + 1 if s % 2 else i - 1
            if 0 <= to < plan.spaces:
                pairs.append((i * plan.scens + s, to * plan.scens + (s ^ 1)))
            else:
                pairs.append((i * plan.scens + s, i * plan.scens + (s ^ 2 if plan.scens % 4 == 0 else s)))
    return pairs


def control_of(plan, cone_list, node_list, probability):
    core = lax.axis_index("scen") % 2
    edge = core * (plan.tiles - 1)
    inner = 1 + core * (plan.tiles - 3)
    local = cone_list - lax.axis_index("space") * plan.tiles
    row_e = lax.dynamic_index_in_dim(local, edge, 0, keepdims=False)
    row_n = lax.dynamic_index_in_dim(local, inner, 0, keepdims=False)
    slot_in = jnp.where(row_e[1] == inner, 1, 2)
    slot_out = 3 - slot_in
    end = (jnp.where(slot_out == 1, row_e[1], row_e[2]) == edge).astype(jnp.int32)
    slot_edge = jnp.where(row_n[1] == edge, 1, 2)
    base = (lax.axis_index("scen") // 2) * plan.local
    nodes = lax.dynamic_slice_in_dim(node_list, base, plan.local, 1).reshape(-1)
    head = jnp.stack([core, edge, inner, slot_in, slot_out, end, slot_edge, 3 - slot_edge]).astype(jnp.int32)
    rows = [probability / jnp.sum(probability)]
    for row in range(2):
        same = node_list[row][:, None] == node_list[row][None, :]
        rows.append(probability / jnp.sum(jnp.where(same, probability[None, :], 0.0), axis=1))
    weights = lax.dynamic_slice_in_dim(jnp.stack(rows), base, plan.local, 1).reshape(-1)
    return jnp.concatenate([head, nodes]), weights


def tiled(plan, start, ore, dual, patterns, cone_list, node_list, probability):
    core = (lax.axis_index("scen") % 2).astype(jnp.int32)
    place = jnp.stack([core, core * (plan.tiles - 1), 1 + core * (plan.tiles - 3)])
    control, weights = control_of(plan, cone_list, node_list, probability)
    flip = [(i, i ^ 1) for i in range(plan.scens)]
    edges = partners(plan)
    swap = lambda x: lax.ppermute(x, "scen", flip)
    outer = lambda x: lax.ppermute(x, AXES, edges)
    half = (2, plan.rank, plan.periods, TILE)
    sums = (plan.blocks, SUB, 2 * TILE)
    chains = plan.chains
    rows = [plan.local * (hi - lo) for lo, hi in chains]
    part = lambda f, *a: functools.partial(f, plan, *a)

    def across(x, stop):
        bits = [1 << b for b in range(1, plan.scens.bit_length() - 1)]
        other = None
        for n, bit in enumerate(bits):
            if n:
                x = x + other
            other = lax.ppermute(x, "scen", [(i, i ^ bit) for i in range(plan.scens)])
        return x, (jnp.zeros_like(x) if other is None else other)

    came = swap(call(part(send_fraction), "send_fraction", [place], [start], [(half, bf16)])[0])
    drive_came = swap(call(part(send_drive), "send_drive", [place], [ore, dual], [(half, f32)])[0])
    n_avg = sum(plan.averaged(c) for c in chains)
    got = call(
        part(start_kernel), "start", [control, weights], [start, came],
        [((r, TILE), f32) for r in rows for _ in range(2)] + [((r, TILE), bf16) for r in rows for _ in range(2)] + [(sums, f32)] * n_avg,
    )
    n = len(chains)
    state = [list(got[2 * c : 2 * c + 2]) for c in range(n)]
    rounded = [list(got[2 * n + 2 * c : 2 * n + 2 * c + 2]) for c in range(n)]
    halo = [[outer(rounded[c][0]), swap(rounded[c][1])] for c in range(n)]
    means = across(sum(got[4 * n + 1 :], got[4 * n]), 0)
    got = call(part(drive_kernel), "drive", [control], [ore, dual, drive_came], [((r, TILE), f32) for r in rows for _ in range(2)])
    drive = [list(got[2 * c : 2 * c + 2]) for c in range(n)]
    moved, pull = [None] * n, [None] * n
    sent = [[None, None] for _ in range(n)]
    for step in range(ITERS * PG_STEPS):
        first = step % PG_STEPS == 0
        closing = step % PG_STEPS == PG_STEPS - 1
        final = step == ITERS * PG_STEPS - 1
        last_round = step >= PG_STEPS
        sums_now = []
        for c, chain in enumerate(chains):
            averaged = plan.averaged(chain)
            shape = (rows[c], TILE)
            quart = (plan.rank * (chain[1] - chain[0]), TILE)
            arrays = [*state[c], halo[c][1], *(drive if first else pull)[c], patterns]
            outs = [(shape, f32), (shape, f32), (shape, bf16)]
            if first:
                arrays += list(means) if averaged else []
                outs += [(shape, f32)] * 2
                outs += [(shape, f32)] * 2 if last_round and averaged else []
            outs += [(quart, f32)] if final else []
            got = call(part(inside, chain, first, last_round, final), f"inside_{step}_{c}", [control], arrays, outs)
            base, state[c][1], rounded_n = got[:3]
            if first:
                pull[c] = list(got[3:5])
                if last_round and averaged:
                    moved[c] = list(got[5:7])
            if final:
                sent[c][1] = swap(got[-1])
            else:
                halo_n = swap(rounded_n)
            with_means = closing and averaged
            arrays = [base, halo[c][0], rounded[c][0], patterns] + ([state[c][1]] if with_means else [])
            outs = [(shape, f32), (shape, bf16)] + ([(sums, f32)] if with_means else []) + ([(quart, f32)] if final else [])
            got = call(part(outside, chain, with_means, final), f"outside_{step}_{c}", [control, weights], arrays, outs)
            state[c][0], rounded[c][0] = got[:2]
            if with_means:
                sums_now.append(got[2])
            if final:
                sent[c][0] = swap(got[-1])
            else:
                halo[c] = [outer(rounded[c][0]), halo_n]
        if closing:
            means = across(sum(sums_now[1:], sums_now[0]), 0)
    count = lambda c: plan.rank * (chains[c][1] - chains[c][0])
    theirs = (swap(means[0]), swap(means[1]))
    arrays = [dual, *means, *theirs]
    for c in range(n):
        arrays += state[c] + sent[c]
        if plan.averaged(chains[c]):
            rest = [lax.dynamic_slice_in_dim(m, (1 - core) * count(c), count(c), 0) for m in moved[c]]
            arrays += moved[c] + [swap(m) for m in rest]
    whole = start.shape
    return tuple(call(part(finish_kernel), "finish", [control], arrays, [(whole, f32), (whole, f32)]))


def solution(mesh):
    def body(start, ore, dual, patterns, cone_list, node_list, probability):
        plan = Plan(mesh, start, cone_list, node_list)
        assert plan.tiles == 4 and plan.scens % 2 == 0 and plan.periods % SUB == 0
        return tiled(plan, start, ore, dual, patterns, cone_list, node_list, probability)

    split = P("scen", None, "space")
    in_specs = (split, split, split, P(), P("space", None), P(), P())
    return jax.shard_map(body, mesh=mesh, in_specs=in_specs, out_specs=(split, split), check_vma=False)
```

```python
import functools
import jax
import jax.numpy as jnp
from jax import lax
from jax.experimental import pallas as pl
from jax.experimental.pallas import tpu as pltpu
from jax.sharding import PartitionSpec as P

TILE = 512
SECTIONS = 4
NODES1 = 4
NODES2 = 16
ITERS = 2
PG_STEPS = 2
SUB = 8
AXES = ("space", "scen")
CHAINS = ((0, 24),)
HALF = 0.5
VMEM_LIMIT = 8 << 20

f32, bf16 = jnp.float32, jnp.bfloat16
HBM = pl.BlockSpec(memory_space=pltpu.HBM)
VMEM = pl.BlockSpec(memory_space=pltpu.VMEM)
LANE = 128
SLOT_IN, SLOT_OUT, END, SLOT_EDGE, SLOT_OTHER = range(5)


def call(kernel, arrays, out, far=(), scratch=(), after=()):
    held = len(far) + len(arrays)

    def body(*refs):
        kernel(*refs[:held], *refs[held + len(after) :])

    return pl.pallas_call(
        body,
        out_shape=[jax.ShapeDtypeStruct(s, d) for s, d in out],
        in_specs=[HBM] * len(far) + [VMEM] * (len(arrays) + len(after)),
        out_specs=[VMEM] * len(out),
        scratch_shapes=list(scratch),
        compiler_params=pltpu.CompilerParams(vmem_limit_bytes=VMEM_LIMIT),
    )(*(pltpu.with_memory_space_constraint(x, pltpu.HBM) for x in far), *arrays, *after)


def lanes(tile):
    return pl.ds(pl.multiple_of(tile * TILE, TILE), TILE)


class Plan:
    def __init__(self, mesh, fraction, cone_list, node_list):
        self.spaces, self.scens = mesh.shape["space"], mesh.shape["scen"]
        self.rank, self.periods, width = fraction.shape
        self.tiles = cone_list.shape[0]
        self.quarter = self.periods // SECTIONS
        self.local = 2 * self.rank
        self.total = node_list.shape[1]
        self.second = self.total > NODES2
        self.blocks = 1 + NODES1 + (NODES2 if self.second else 0)
        self.reach = (3 if self.second else 2) * self.quarter
        self.groups = -(-self.reach // SUB)
        self.chains = CHAINS

    def averaged(self, chain):
        return chain[0] < self.reach

    def section_of(self, block):
        return 0 if block == 0 else 1 if block <= NODES1 else 2

    def meets(self, low, section):
        return low < (section + 1) * self.quarter and low + SUB > section * self.quarter

    def blocks_at(self, low):
        return [b for b in range(self.blocks) if self.meets(low, self.section_of(b))]

    def core(self):
        return lax.axis_index("scen") % 2

    def edge_of(self, core):
        return core * (self.tiles - 1)

    def inner_of(self, core):
        return 1 + core * (self.tiles - 3)


def rows_from(start, count):
    return pl.ds(pl.multiple_of(start, SUB), count)


def prepare_kernel(plan, *refs):
    small_far, (start, ore, dual) = refs[:3], refs[3:6]
    held, drive, drive_sent, control, share, select = refs[6:12]
    ores, duals, *small, sems = refs[12:]
    core = plan.core()
    copies = []
    for source, target in zip(small_far, small):
        copies.append(pltpu.make_async_copy(source, target, sems.at[len(copies)]))
    for k in range(2):
        for which, at in enumerate((core, 1 - core)):
            tile = (plan.edge_of, plan.inner_of)[k](at)
            fetch = [(ore, ores.at[which, k]), (dual, duals.at[which, k])] + ([(start, held.at[k])] if which == 0 else [])
            for source, target in fetch:
                copies.append(pltpu.make_async_copy(source.at[:, :, lanes(tile)], target, sems.at[len(copies)]))
    for copy in copies:
        copy.start()
    for copy in copies[: len(small)]:
        copy.wait()
    cones, nodes, chances = small
    edge, inner = plan.edge_of(core), plan.inner_of(core)
    base = lax.axis_index("space") * plan.tiles
    slot_in = jnp.where(cones[edge, 1] == base + inner, 1, 2)
    slot_out = 3 - slot_in
    end = jnp.where(cones[edge, slot_out] == base + edge, 1, 0)
    slot_edge = jnp.where(cones[inner, 1] == base + edge, 1, 2)
    place = lax.broadcasted_iota(jnp.int32, (SUB, LANE), 1)
    vector = jnp.zeros((SUB, LANE), jnp.int32)
    for k, v in enumerate((slot_in, slot_out, end, slot_edge, 3 - slot_edge)):
        vector = jnp.where(place == k, v, vector)
    control[...] = vector
    first = (lax.axis_index("scen") // 2) * plan.local
    splat = lambda v: jnp.full((SUB, LANE), v, f32)
    sections = 3 if plan.second else 2
    for j in range(plan.local):
        mine = first + j
        weights = []
        for section in range(sections):
            total = jnp.float32(0)
            for other in range(plan.total):
                chance = chances[other]
                if section:
                    chance = jnp.where(nodes[section - 1, other] == nodes[section - 1, mine], chance, 0.0)
                total = total + chance
            weights.append(splat(chances[mine]) / splat(total))
        for group in range(plan.groups):
            period = group * SUB + lax.broadcasted_iota(jnp.int32, (SUB, LANE), 0)
            for block in plan.blocks_at(group * SUB):
                section = plan.section_of(block)
                inside = (period >= section * plan.quarter) & (period < (section + 1) * plan.quarter)
                chosen = jnp.where(inside, 1.0, 0.0)
                if section:
                    node = block - (1 if section == 1 else 1 + NODES1)
                    chosen = chosen * jnp.where(nodes[section - 1, mine] == node, 1.0, 0.0)
                select[group, block, j] = chosen
                share[group, block, j] = chosen * weights[section]
    for copy in copies[len(small) :]:
        copy.wait()
    for k in range(2):
        drive[k] = ores[0, k].astype(f32) - duals[0, k]
        drive_sent[k] = ores[1, k].astype(f32) - duals[1, k]


def means_of_tile(plan, chain, share, source, sums, sent):
    lo, hi = chain
    size = hi - lo
    for chunk in range(TILE // LANE):
        span = slice(chunk * LANE, (chunk + 1) * LANE)
        totals = [jnp.zeros((SUB, LANE), f32)] * plan.blocks
        for low in range(lo, min(hi, plan.reach), SUB):
            for j in range(plan.local):
                row = j * size + low - lo
                value = source[row : row + SUB, span] - HALF
                for block in plan.blocks_at(low):
                    totals[block] = totals[block] + share[low // SUB, block, j] * value
        for block in range(plan.blocks):
            sums[block, :, span] = totals[block]
            sent[block, :, span] = totals[block].astype(bf16)


def means_kernel(plan, chain, final, share, *refs):
    count = (len(refs) - final) // 3
    for k in range(count):
        means_of_tile(plan, chain, share, refs[k], refs[count + k], refs[2 * count + k])
    if final:
        source, sums, packed = refs[0], refs[1], refs[-1]
        rows = plan.rank * (chain[1] - chain[0])
        packed[:rows, :] = other_rows(plan, chain, source)
        for block in range(plan.blocks):
            packed[rows + block * SUB : rows + (block + 1) * SUB, :] = sums[block]


def whole_means(plan, pair, span):
    return [pair[0][b, :, span] + pair[1][b, :, span].astype(f32) + HALF for b in range(plan.blocks)]


def center_rows(plan, low, j, select, means, value):
    if low >= plan.reach:
        return value
    mean = jnp.zeros_like(value)
    for block in plan.blocks_at(low):
        mean = mean + select[low // SUB, block, j] * means[block]
    if low + SUB > plan.reach:
        period = low + lax.broadcasted_iota(jnp.int32, value.shape, 0)
        mean = jnp.where(period < plan.reach, mean, value)
    return mean


def assemble(plan, own, theirs, out):
    core = plan.core()
    for (lo, hi), pair in zip(plan.chains, out):
        size = hi - lo
        for k, ref in enumerate(pair):
            for r in range(plan.rank):
                ref[rows_from((core * plan.rank + r) * size, size), :] = own(k, r, lo, hi).astype(f32)
                ref[rows_from(((1 - core) * plan.rank + r) * size, size), :] = theirs(k, r, lo, hi).astype(f32)


def start_kernel(plan, held, came, *outs):
    n = len(plan.chains)
    state = [outs[2 * c : 2 * c + 2] for c in range(n)]
    sends = [outs[2 * n + 2 * c : 2 * n + 2 * c + 2] for c in range(n)]
    tiles = (plan.edge_of(plan.core()), plan.inner_of(plan.core()))
    assemble(plan, lambda k, r, lo, hi: held[k, r, lo:hi, :], lambda k, r, lo, hi: came[r, lo:hi, lanes(tiles[k])], state)
    for pair, send in zip(state, sends):
        for ref, out in zip(pair, send):
            out[...] = ref[...].astype(bf16)


def drive_kernel(plan, held, came, *outs):
    take = lambda ref: lambda k, r, lo, hi: ref[k, r, lo:hi, :]
    assemble(plan, take(held), take(came), [outs[2 * c : 2 * c + 2] for c in range(len(plan.chains))])


def other_rows(plan, chain, ref):
    count = plan.rank * (chain[1] - chain[0])
    return ref[rows_from((1 - plan.core()) * count, count), :]


def inside_kernel(plan, chain, first, last_round, final, control, edge, inner, halo, drive_e, drive_n, patterns, *rest):
    lo, hi = chain
    size = hi - lo
    averaged = plan.averaged(chain)
    rest = list(rest)
    pull_e, pull_n = drive_e, drive_n
    if first and averaged:
        select = rest.pop(0)
        means_refs = [(rest.pop(0), rest.pop(0)) for _ in range(2)]
    base_e, next_n = rest[:2]
    rest = rest[2:]
    if not final:
        send_n = rest.pop(0)
    if first:
        pull_e, pull_n = rest[:2]
        rest = rest[2:]
        moved = rest[:3] if last_round and averaged else None
        for side, (value, drive, pull) in enumerate(((edge, drive_e, pull_e), (inner, drive_n, pull_n))):
            if not averaged:
                pull[...] = drive[...] + value[...]
                continue
            for chunk in range(TILE // LANE):
                span = slice(chunk * LANE, (chunk + 1) * LANE)
                means = whole_means(plan, means_refs[side], span)
                for j in range(plan.local):
                    for low in range(lo, hi, SUB):
                        rows = slice(j * size + low - lo, j * size + low - lo + SUB)
                        now = value[rows, span]
                        mean = center_rows(plan, low, j, select, means, now)
                        if last_round:
                            gap = now - mean
                            moved[side][rows, span] = gap
                            pull[rows, span] = drive[rows, span] - gap + mean
                        else:
                            pull[rows, span] = drive[rows, span] + mean
        if moved:
            for side in range(2):
                moved[2][side] = other_rows(plan, chain, moved[side])
    round_e, round_n = edge[...].astype(bf16), inner[...].astype(bf16)
    dot = functools.partial(jnp.dot, preferred_element_type=f32)
    cone = dot(round_n, patterns[0]) + dot(round_e, patterns[control[0, SLOT_EDGE]]) + dot(halo[...], patterns[control[0, SLOT_OTHER]])
    value = inner[...]
    value = jnp.clip(value - 0.4 * ((value - cone) + value - pull_n[...]), 0.0, 1.0)
    next_n[...] = value
    if not final:
        send_n[...] = value.astype(bf16)
    cone = dot(round_e, patterns[0]) + dot(round_n, patterns[control[0, SLOT_IN]])
    value = edge[...]
    base_e[...] = value - 0.4 * ((value - cone) + value - pull_e[...])

    @pl.when(control[0, END] == 1)
    def _():
        base_e[...] += 0.4 * dot(round_e, patterns[control[0, SLOT_OUT]])


def outside_kernel(plan, control, base, halo, patterns, next_e, send_e=None):
    scale = 0.4 * (1 - control[0, END]).astype(f32)
    cone = jnp.dot(halo[...], patterns[control[0, SLOT_OUT]], preferred_element_type=f32)
    value = jnp.clip(base[...] + scale * cone, 0.0, 1.0)
    next_e[...] = value
    if send_e is not None:
        send_e[...] = value.astype(bf16)


def front_kernel(plan, dual, *refs):
    refs = list(refs)
    fraction, price = refs[-2:]
    core = plan.core()
    tiles = [(plan.edge_of(c), plan.inner_of(c)) for c in (core, 1 - core)]
    at = 0
    for lo, hi in plan.chains:
        size = hi - lo
        held, came = refs[at : at + 2], refs[at + 2 : at + 4]
        at += 4
        averaged = plan.averaged((lo, hi))
        if averaged:
            moved, moved_came = refs[at : at + 2], refs[at + 2]
            at += 3
        for part in range(2):
            for side in range(2):
                for r in range(plan.rank):
                    if part == 0:
                        rows, value, gap = rows_from((core * plan.rank + r) * size, size), held[side], averaged and moved[side]
                    else:
                        rows, value, gap = slice(r * size, (r + 1) * size), came[side], averaged and moved_came.at[side]
                    out = (r, slice(lo, hi), lanes(tiles[part][side]))
                    now, first = value[rows, :], dual[out]
                    fraction[out] = now
                    if averaged:
                        period = lo + lax.broadcasted_iota(jnp.int32, now.shape, 0)
                        first = jnp.where(period < plan.reach, first + gap[rows, :] + now, first)
                    price[out] = first


def finish_kernel(plan, offset, price, select, *refs):
    pairs = [[(refs[4 * p + 2 * s], refs[4 * p + 2 * s + 1]) for s in range(2)] for p in range(2)]
    out = refs[-1]
    core = plan.core()
    tiles = [(plan.edge_of(c), plan.inner_of(c)) for c in (core, 1 - core)]
    top = plan.groups * SUB
    if top < plan.periods:
        out[:, top:, :] = price[:, top:, :]
    for part in range(2):
        for side in range(2):
            for chunk in range(TILE // LANE):
                span = slice(chunk * LANE, (chunk + 1) * LANE)
                first, second = pairs[part][side]
                if part and offset:
                    first = [first[offset + b * SUB : offset + (b + 1) * SUB, span] for b in range(plan.blocks)]
                    means = [first[b] + second[b, :, span].astype(f32) + HALF for b in range(plan.blocks)]
                else:
                    means = whole_means(plan, (first, second), span)
                where = pl.ds(pl.multiple_of(tiles[part][side] * TILE + chunk * LANE, LANE), LANE)
                for r in range(plan.rank):
                    for low in range(0, top, SUB):
                        value = price[r, low : low + SUB, where]
                        for block in plan.blocks_at(low):
                            value = value - select[low // SUB, block, core * plan.rank + r] * means[block]
                        out[r, low : low + SUB, where] = value


def partners(plan):
    pairs = []
    for i in range(plan.spaces):
        for s in range(plan.scens):
            to = i + 1 if s % 2 else i - 1
            if 0 <= to < plan.spaces:
                pairs.append((i * plan.scens + s, to * plan.scens + (s ^ 1)))
            else:
                pairs.append((i * plan.scens + s, i * plan.scens + (s ^ 2 if plan.scens % 4 == 0 else s)))
    return pairs


def tiled(plan, start, ore, dual, patterns, cone_list, node_list, probability):
    flip = [(i, i ^ 1) for i in range(plan.scens)]
    edges = partners(plan)

    swap = lambda x: lax.ppermute(x, "scen", flip)
    outer = lambda x: lax.ppermute(x, AXES, edges)
    half = (2, plan.rank, plan.periods, TILE)
    sums = (plan.blocks, SUB, TILE)
    shares = (plan.groups, plan.blocks, plan.local, SUB, LANE)
    chains = plan.chains
    n = len(chains)
    rows = [plan.local * (hi - lo) for lo, hi in chains]
    part = lambda f, *a: functools.partial(f, plan, *a)
    ranks = range(n)
    pairs = lambda kind: [((r, TILE), kind) for r in rows for _ in range(2)]
    bits = [1 << b for b in range(1, plan.scens.bit_length() - 1)]
    jump = lambda x, bit: lax.ppermute(x, "scen", [(i, i ^ bit) for i in range(plan.scens)])

    def across(x, sent):
        other = None
        for k, bit in enumerate(bits):
            if k:
                x = x + other.astype(f32)
                sent = x.astype(bf16)
            other = jump(sent, bit)
        return x, (jnp.zeros_like(sent) if other is None else other), sent

    def means_of(sides, final=False, after=()):
        count = len(sides)
        total = None
        for c in ranks:
            if plan.averaged(chains[c]):
                arrays = [share, *(state[c][k] for k in sides)]
                outs = [(sums, f32)] * count + [(sums, bf16)] * count
                outs += [((plan.rank * (chains[c][1] - chains[c][0]) + plan.blocks * SUB, TILE), f32)] if final else []
                got = call(part(means_kernel, chains[c], final), arrays, outs, after=after)
                got = list(got)
                if final:
                    sent[c][sides[0]] = got.pop()
                if total is not None:
                    got = [g + t for g, t in zip(got[:count], total)]
                    got += [g.astype(bf16) for g in got]
                total = got
        return [across(total[k], total[count + k]) for k in range(count)]

    came = swap(start)
    parts = (2, 2, plan.rank, plan.periods, TILE)
    held, drive_held, drive_sent, control, share, select = call(
        part(prepare_kernel), [],
        [(half, bf16), (half, f32), (half, f32), ((SUB, LANE), jnp.int32), (shares, f32), (shares, f32)],
        far=[cone_list, node_list, probability, start, ore, dual],
        scratch=[
            pltpu.VMEM(parts, bf16),
            pltpu.VMEM(parts, f32),
            *(pltpu.SMEM(x.shape, x.dtype) for x in (cone_list, node_list, probability)),
            pltpu.SemaphoreType.DMA((13,)),
        ],
    )
    got = call(part(start_kernel), [held, came], pairs(f32) + pairs(bf16))
    state = [list(got[2 * c : 2 * c + 2]) for c in ranks]
    rounded = [list(got[2 * n + 2 * c : 2 * n + 2 * c + 2]) for c in ranks]
    halo = [[outer(rounded[c][0]), swap(rounded[c][1])] for c in ranks]
    means = means_of((0, 1))
    drive_came = swap(drive_sent)
    got = call(part(drive_kernel), [drive_held, drive_came], pairs(f32))
    drive = [list(got[2 * c : 2 * c + 2]) for c in ranks]
    moved, pull = [None] * n, [None] * n
    sent = [[None, None] for _ in ranks]
    last = []
    for step in range(ITERS * PG_STEPS):
        first = step % PG_STEPS == 0
        closing = step % PG_STEPS == PG_STEPS - 1
        final = step == ITERS * PG_STEPS - 1
        last_round = step >= PG_STEPS
        base, halo_n = [None] * n, [None] * n
        order = sorted(ranks, key=lambda c: first and plan.averaged(chains[c]))
        for c in order:
            chain = chains[c]
            averaged = plan.averaged(chain)
            shape = (rows[c], TILE)
            quart = (2, plan.rank * (chain[1] - chain[0]), TILE)
            arrays = [control, *state[c], halo[c][1], *(drive if first else pull)[c], patterns]
            outs = [(shape, f32), (shape, f32)] + ([] if final else [(shape, bf16)])
            if first:
                arrays += [select, *means[0][:2], *means[1][:2]] if averaged else []
                outs += [(shape, f32)] * 2
                outs += [(shape, f32)] * 2 + [(quart, f32)] if last_round and averaged else []
            got = call(part(inside_kernel, chain, first, last_round, final), arrays, outs, after=last)
            last = [got[0]]
            base[c], state[c][1] = got[:2]
            if first:
                pull[c] = list(got[3:5])
                if last_round and averaged:
                    moved[c] = [*got[5:7], swap(got[7])]
            if not final:
                halo_n[c] = swap(got[2])
        if closing:
            means_n = means_of((1,), final)
            last = [means_n[0][2]]
        for c in ranks:
            chain = chains[c]
            shape = (rows[c], TILE)
            outs = [(shape, f32)] + ([] if final else [(shape, bf16)])
            got = call(part(outside_kernel), [control, base[c], halo[c][0], patterns], outs, after=last)
            last = [got[0]]
            state[c][0] = got[0]
            if not final:
                halo[c] = [outer(got[1]), halo_n[c]]
            if closing and c == max(k for k in ranks if plan.averaged(chains[k])):
                means = means_of((0,), final) + means_n
    averaged = [c for c in ranks if plan.averaged(chains[c])]
    packed = len(averaged) == 1 and len(bits) == 1
    for c in ranks:
        if plan.averaged(chains[c]):
            sent[c] = [swap(x) for x in sent[c]]
        else:
            count = plan.rank * (chains[c][1] - chains[c][0])
            sent[c] = [swap(call(lambda x, o, c=c: o.__setitem__(..., other_rows(plan, chains[c], x)), [x], [((count, TILE), f32)])[0]) for x in state[c]]
    theirs = [(sent[averaged[0]][k] if packed else swap(means[k][0]), swap(means[k][1])) for k in range(2)]
    arrays = [dual]
    for c in ranks:
        arrays += state[c] + sent[c] + (moved[c] if plan.averaged(chains[c]) else [])
    fraction, price = call(part(front_kernel), arrays, [(start.shape, f32)] * 2)
    arrays = [price, select, *means[0][:2], *means[1][:2], *theirs[0], *theirs[1]]
    offset = plan.rank * (chains[averaged[0]][1] - chains[averaged[0]][0]) if packed else 0
    return fraction, call(part(finish_kernel, offset), arrays, [(start.shape, f32)])[0]


def solution(mesh):
    def body(start, ore, dual, patterns, cone_list, node_list, probability):
        plan = Plan(mesh, start, cone_list, node_list)
        assert plan.tiles == 4 and plan.scens % 2 == 0 and plan.periods % SUB == 0
        return tiled(plan, start, ore, dual, patterns, cone_list, node_list, probability)

    split = P("scen", None, "space")
    in_specs = (split, split, split, P(), P("space", None), P(), P())
    return jax.shard_map(body, mesh=mesh, in_specs=in_specs, out_specs=(split, split), check_vma=False)
```

```python
import functools
import jax
import jax.numpy as jnp
from jax import lax
from jax.experimental import pallas as pl
from jax.experimental.pallas import tpu as pltpu
from jax.sharding import PartitionSpec as P

TILE = 512
SECTIONS = 4
NODES1 = 4
NODES2 = 16
ITERS = 2
PG_STEPS = 2
SUB = 8
AXES = ("space", "scen")
HALF = 0.5
VMEM_LIMIT = 8 << 20

f32, bf16 = jnp.float32, jnp.bfloat16
HBM = pl.BlockSpec(memory_space=pltpu.HBM)
VMEM = pl.BlockSpec(memory_space=pltpu.VMEM)
LANE = 128
SLOT_IN, SLOT_OUT, END, SLOT_EDGE, SLOT_OTHER = range(5)


def call(kernel, arrays, out, far=(), scratch=(), after=(), far_out=False):
    held = len(far) + len(arrays)

    def body(*refs):
        kernel(*refs[:held], *refs[held + len(after) :])

    return pl.pallas_call(
        body,
        out_shape=[jax.ShapeDtypeStruct(s, d) for s, d in out],
        in_specs=[HBM] * len(far) + [VMEM] * (len(arrays) + len(after)),
        out_specs=[HBM if far_out else VMEM] * len(out),
        scratch_shapes=list(scratch),
        compiler_params=pltpu.CompilerParams(vmem_limit_bytes=VMEM_LIMIT),
    )(*(pltpu.with_memory_space_constraint(x, pltpu.HBM) for x in far), *arrays, *after)


def lanes(tile):
    return pl.ds(pl.multiple_of(tile * TILE, TILE), TILE)


def rows_from(start, count):
    return pl.ds(pl.multiple_of(start, SUB), count)


class Plan:
    def __init__(self, mesh, fraction, cone_list, node_list):
        self.spaces, self.scens = mesh.shape["space"], mesh.shape["scen"]
        self.rank, self.periods, self.width = fraction.shape
        self.tiles = cone_list.shape[0]
        self.quarter = self.periods // SECTIONS
        self.local = 2 * self.rank
        self.total = node_list.shape[1]
        self.second = self.total > NODES2
        self.blocks = 1 + NODES1 + (NODES2 if self.second else 0)
        self.reach = (3 if self.second else 2) * self.quarter
        self.groups = -(-self.reach // SUB)
        self.top = self.groups * SUB
        self.parts = [(0, self.periods)]
        self.rows = self.local * self.periods
        self.own = self.rank * self.periods

    def part_of(self, low):
        return [low >= lo and low < hi for lo, hi in self.parts].index(True)

    def row(self, j, low, scenarios):
        lo, hi = self.parts[self.part_of(low)]
        return scenarios * lo + j * (hi - lo) + low - lo

    def section_of(self, block):
        return 0 if block == 0 else 1 if block <= NODES1 else 2

    def meets(self, low, section):
        return low < (section + 1) * self.quarter and low + SUB > section * self.quarter

    def blocks_at(self, low):
        return [b for b in range(self.blocks) if self.meets(low, self.section_of(b))]

    def core(self):
        return lax.axis_index("scen") % 2

    def edge_of(self, core):
        return core * (self.tiles - 1)

    def inner_of(self, core):
        return 1 + core * (self.tiles - 3)


class Rows:
    def __init__(self, plan, *refs):
        self.plan, self.refs = plan, refs

    def place(self, j, low):
        row = self.plan.row(j, low, self.plan.local)
        if len(self.refs) == 1:
            return self.refs[0], row
        part = self.plan.part_of(low)
        return self.refs[part], row - self.plan.local * self.plan.parts[part][0]

    def read(self, j, low, span):
        ref, row = self.place(j, low)
        return ref[rows_from(row, SUB), span]

    def all(self):
        return self.refs[0][...] if len(self.refs) == 1 else jnp.concatenate([ref[...] for ref in self.refs], axis=0)


def other_rows(plan, rows, out, parts=None):
    other = (1 - plan.core()) * plan.rank
    for part in range(len(plan.parts)) if parts is None else parts:
        lo, hi = plan.parts[part]
        count = plan.rank * (hi - lo)
        ref, row = rows.place(other, lo)
        at = plan.rank * lo if parts is None else 0
        out[at : at + count, :] = ref[rows_from(row, count), :]


def prepare_kernel(plan, *refs):
    small_far, (start, ore, dual) = refs[:3], refs[3:6]
    held, drive, drive_sent, control, share, select = refs[6:12]
    ores, duals, *small, sems = refs[12:]
    core = plan.core()
    copies = []
    for source, target in zip(small_far, small):
        copies.append(pltpu.make_async_copy(source, target, sems.at[len(copies)]))
    for k in range(2):
        for which, at in enumerate((core, 1 - core)):
            tile = (plan.edge_of, plan.inner_of)[k](at)
            fetch = [(ore, ores.at[which, k]), (dual, duals.at[which, k])] + ([(start, held.at[k])] if which == 0 else [])
            for source, target in fetch:
                copies.append(pltpu.make_async_copy(source.at[:, :, lanes(tile)], target, sems.at[len(copies)]))
    for copy in copies:
        copy.start()
    for copy in copies[: len(small)]:
        copy.wait()
    cones, nodes, chances = small
    edge, inner = plan.edge_of(core), plan.inner_of(core)
    base = lax.axis_index("space") * plan.tiles
    slot_in = jnp.where(cones[edge, 1] == base + inner, 1, 2)
    slot_out = 3 - slot_in
    end = jnp.where(cones[edge, slot_out] == base + edge, 1, 0)
    slot_edge = jnp.where(cones[inner, 1] == base + edge, 1, 2)
    place = lax.broadcasted_iota(jnp.int32, (SUB, LANE), 1)
    vector = jnp.zeros((SUB, LANE), jnp.int32)
    for k, v in enumerate((slot_in, slot_out, end, slot_edge, 3 - slot_edge)):
        vector = jnp.where(place == k, v, vector)
    control[...] = vector
    first = (lax.axis_index("scen") // 2) * plan.local
    splat = lambda v: jnp.full((SUB, LANE), v, f32)
    within = []
    for block in range(plan.blocks):
        section = plan.section_of(block)
        node = block - (1 if section == 1 else 1 + NODES1)
        total = jnp.float32(0)
        for other in range(plan.total):
            chance = chances[other]
            total = total + (jnp.where(nodes[section - 1, other] == node, chance, 0.0) if section else chance)
        within.append(1.0 / splat(total))
    for group in range(plan.groups):
        period = group * SUB + lax.broadcasted_iota(jnp.int32, (SUB, LANE), 0)
        for block in plan.blocks_at(group * SUB):
            section = plan.section_of(block)
            node = block - (1 if section == 1 else 1 + NODES1)
            inside = (period >= section * plan.quarter) & (period < (section + 1) * plan.quarter)
            mask = jnp.where(inside, 1.0, 0.0)
            for j in range(plan.local):
                chosen = mask
                if section:
                    chosen = mask * jnp.where(nodes[section - 1, first + j] == node, 1.0, 0.0)
                select[group, block, j] = chosen
                share[group, block, j] = chosen * (within[block] * chances[first + j])
    for copy in copies[len(small) :]:
        copy.wait()
    for k in range(2):
        drive[k] = ores[0, k].astype(f32) - duals[0, k]
        drive_sent[k] = ores[1, k].astype(f32) - duals[1, k]


def means_of_tile(plan, share, source, sums, sent):
    for chunk in range(TILE // LANE):
        span = slice(chunk * LANE, (chunk + 1) * LANE)
        totals = [jnp.zeros((SUB, LANE), f32)] * plan.blocks
        for low in range(0, plan.top, SUB):
            for j in range(plan.local):
                value = source.read(j, low, span) - HALF
                for block in plan.blocks_at(low):
                    totals[block] = totals[block] + share[low // SUB, block, j] * value
        for block in range(plan.blocks):
            sums[block, :, span] = totals[block]
            if sent is not None:
                sent[block, :, span] = totals[block].astype(bf16)


def means_kernel(plan, short, final, share, *refs):
    count = (len(refs) - final) // (3 if short else 2)
    for k in range(count):
        means_of_tile(plan, share, Rows(plan, refs[k]), refs[count + k], refs[2 * count + k] if short else None)
    if final:
        source, sums, packed = refs[0], refs[1], refs[-1]
        other_rows(plan, Rows(plan, source), packed, None if source.shape[0] == plan.rows else [0])
        first = packed.shape[0] - plan.blocks * SUB
        for block in range(plan.blocks):
            packed[first + block * SUB : first + (block + 1) * SUB, :] = sums[block]


def whole_means(plan, pair, span):
    return [pair[0][b, :, span] + pair[1][b, :, span].astype(f32) + HALF for b in range(plan.blocks)]


def center_rows(plan, low, j, select, means, value):
    mean = jnp.zeros_like(value)
    for block in plan.blocks_at(low):
        mean = mean + select[low // SUB, block, j] * means[block]
    if low + SUB > plan.reach:
        period = low + lax.broadcasted_iota(jnp.int32, value.shape, 0)
        mean = jnp.where(period < plan.reach, mean, value)
    return mean


def assemble(plan, own, theirs, out):
    core = plan.core()
    for k, rows in enumerate(out):
        for r in range(plan.rank):
            for lo, hi in plan.parts:
                for at, source in ((core, own), (1 - core, theirs)):
                    ref, row = rows.place(at * plan.rank + r, lo)
                    ref[rows_from(row, hi - lo), :] = source(k, r, lo, hi).astype(f32)


def start_kernel(plan, held, came, *outs):
    n = len(plan.parts)
    tiles = (plan.edge_of(plan.core()), plan.inner_of(plan.core()))
    state, sends = outs[: n + 1], outs[n + 1 :]
    out = (Rows(plan, *state[:n]), Rows(plan, state[n]))
    assemble(plan, lambda k, r, lo, hi: held[k, r, lo:hi, :], lambda k, r, lo, hi: came[r, lo:hi, lanes(tiles[k])], out)
    for ref, send in zip(state, sends):
        send[...] = ref[...].astype(bf16)


def drive_kernel(plan, held, came, drive_e, drive_n):
    take = lambda ref: lambda k, r, lo, hi: ref[k, r, lo:hi, :]
    assemble(plan, take(held), take(came), (Rows(plan, drive_e), Rows(plan, drive_n)))


def cones(control, edge, inner, halo, patterns):
    round_e, round_n = edge.all().astype(bf16), inner[...].astype(bf16)
    dot = functools.partial(jnp.dot, preferred_element_type=f32)
    cone_n = dot(round_n, patterns[0]) + dot(round_e, patterns[control[0, SLOT_EDGE]]) + dot(halo[...], patterns[control[0, SLOT_OTHER]])
    return dot(round_e, patterns[0]) + dot(round_n, patterns[control[0, SLOT_IN]]), cone_n


def own_outside(control, edge, patterns):
    return jnp.dot(edge.all().astype(bf16), patterns[control[0, SLOT_OUT]], preferred_element_type=f32)


def stepped(value, cone, pull):
    return value - 0.4 * ((value - cone) + value - pull)


def cone_kernel(plan, control, *refs):
    *edges, inner, halo, patterns, cone_e, cone_n = refs
    edge = Rows(plan, *edges)
    cone_e[...], cone_n[...] = cones(control, edge, inner, halo, patterns)

    @pl.when(control[0, END] == 1)
    def _():
        cone_e[...] += own_outside(control, edge, patterns)


def center_kernel(plan, last_round, *refs):
    n = len(plan.parts)
    edge, inner = Rows(plan, *refs[:n]), Rows(plan, refs[n])
    cone_e, cone_n, drive_e, drive_n, select = refs[n + 1 : n + 6]
    means_refs = (refs[n + 6 : n + 8], refs[n + 8 : n + 10])
    base_e, next_n, send_n, pull_e, pull_n, *moved = refs[n + 10 :]
    for side, (value, cone, drive, pull) in enumerate(((edge, cone_e, drive_e, pull_e), (inner, cone_n, drive_n, pull_n))):
        for chunk in range(TILE // LANE):
            span = slice(chunk * LANE, (chunk + 1) * LANE)
            means = whole_means(plan, means_refs[side], span)
            for j in range(plan.local):
                for low in range(0, plan.periods, SUB):
                    row = plan.row(j, low, plan.local)
                    rows = slice(row, row + SUB)
                    now = value.read(j, low, span)
                    mean = center_rows(plan, low, j, select, means, now) if low < plan.top else now
                    drawn = drive[rows, span] + mean
                    if last_round and low < plan.top:
                        gap = now - mean
                        moved[side][rows, span] = gap
                        drawn = drawn - gap
                    pull[rows, span] = drawn
                    after = stepped(now, cone[rows, span], drawn)
                    if side == 0:
                        base_e[rows, span] = after
                    else:
                        next_n[rows, span] = jnp.clip(after, 0.0, 1.0)
    send_n[...] = next_n[...].astype(bf16)
    if last_round:
        for side in range(2):
            other_rows(plan, Rows(plan, moved[side]), moved[2].at[side])


def inside_kernel(plan, final, control, *refs):
    n = len(plan.parts)
    edge = Rows(plan, *refs[:n])
    inner, halo, pull_e, pull_n, patterns, base_e, next_n, *send_n = refs[n:]
    cone_e, cone_n = cones(control, edge, inner, halo, patterns)
    value = jnp.clip(stepped(inner[...], cone_n, pull_n[...]), 0.0, 1.0)
    next_n[...] = value
    if not final:
        send_n[0][...] = value.astype(bf16)
    base_e[...] = stepped(edge.all(), cone_e, pull_e[...])

    @pl.when(control[0, END] == 1)
    def _():
        base_e[...] += 0.4 * own_outside(control, edge, patterns)


def outside_kernel(plan, part, control, base, halo, patterns, next_e, *send_e):
    lo, hi = plan.parts[part]
    scale = 0.4 * (1 - control[0, END]).astype(f32)
    cone = jnp.dot(halo[...], patterns[control[0, SLOT_OUT]], preferred_element_type=f32)
    value = jnp.clip(base[plan.local * lo : plan.local * hi, :] + scale * cone, 0.0, 1.0)
    next_e[...] = value
    if send_e:
        send_e[0][...] = value.astype(bf16)


def pick_kernel(plan, source, out):
    lo, hi = plan.parts[1]
    count = plan.rank * (hi - lo)
    out[...] = source[rows_from((1 - plan.core()) * count, count), :]


def own_tiles(plan, side, core):
    return (plan.edge_of, plan.inner_of)[side](core)


def fraction_kernel(plan, *refs):
    n = len(plan.parts)
    held = (Rows(plan, *refs[:n]), Rows(plan, refs[n]))
    packed_n, *packed_e, out = refs[n + 1 :]
    core = plan.core()
    for side in range(2):
        for r in range(plan.rank):
            for part, (lo, hi) in enumerate(plan.parts):
                ref, row = held[side].place(core * plan.rank + r, lo)
                out[r, lo:hi, lanes(own_tiles(plan, side, core))] = ref[rows_from(row, hi - lo), :]
                row = plan.row(r, lo, plan.rank)
                source = packed_n
                if side == 0:
                    source, row = packed_e[part], row - plan.rank * lo
                out[r, lo:hi, lanes(own_tiles(plan, side, 1 - core))] = source[row : row + hi - lo, :]


def price_kernel(plan, dual, edge, inner, packed_e, packed_n, moved_e, moved_n, moved_came, out):
    core = plan.core()
    count = plan.parts[0][1]
    period = lax.broadcasted_iota(jnp.int32, (plan.top, TILE), 0)
    for side, (value, packed, moved) in enumerate(((edge, packed_e, moved_e), (inner, packed_n, moved_n))):
        for r in range(plan.rank):
            own = rows_from((core * plan.rank + r) * count, plan.top)
            came = slice(r * count, r * count + plan.top)
            for at, now, gap in ((core, value[own, :], moved[own, :]), (1 - core, packed[came, :], moved_came[side, came, :])):
                where = lanes(own_tiles(plan, side, at))
                first = dual[r, : plan.top, where]
                out[r, :, where] = jnp.where(period < plan.reach, first + gap + now, first)


def finish_kernel(plan, offsets, dual, price, select, *refs):
    pairs = [[(refs[4 * p + 2 * s], refs[4 * p + 2 * s + 1]) for s in range(2)] for p in range(2)]
    out, made, sems = refs[-3:]
    core = plan.core()
    copies = []
    if plan.top < plan.periods:
        copies.append(pltpu.make_async_copy(dual.at[:, plan.top :, :], out.at[:, plan.top :, :], sems.at[plan.rank]))
        copies[0].start()
    for r in range(plan.rank):
        for owner in range(2):
            for side in range(2):
                tile = own_tiles(plan, side, core if owner == 0 else 1 - core)
                for chunk in range(TILE // LANE):
                    span = slice(chunk * LANE, (chunk + 1) * LANE)
                    first, second = pairs[owner][side]
                    if owner and offsets[side]:
                        first = [first[offsets[side] + b * SUB : offsets[side] + (b + 1) * SUB, span] for b in range(plan.blocks)]
                        means = [first[b] + second[b, :, span].astype(f32) + HALF for b in range(plan.blocks)]
                    else:
                        means = whole_means(plan, (first, second), span)
                    where = pl.ds(pl.multiple_of(tile * TILE + chunk * LANE, LANE), LANE)
                    for low in range(0, plan.top, SUB):
                        value = price[r, low : low + SUB, where]
                        for block in plan.blocks_at(low):
                            value = value - select[low // SUB, block, core * plan.rank + r] * means[block]
                        made[r, low : low + SUB, where] = value
        copy = pltpu.make_async_copy(made.at[r], out.at[r, : plan.top, :], sems.at[r])
        copy.start()
        copies.append(copy)
    for copy in copies:
        copy.wait()


def partners(plan):
    pairs = []
    for i in range(plan.spaces):
        for s in range(plan.scens):
            to = i + 1 if s % 2 else i - 1
            if 0 <= to < plan.spaces:
                pairs.append((i * plan.scens + s, to * plan.scens + (s ^ 1)))
            else:
                pairs.append((i * plan.scens + s, i * plan.scens + (s ^ 2 if plan.scens % 4 == 0 else s)))
    return pairs


def tiled(plan, start, ore, dual, patterns, cone_list, node_list, probability):
    flip = [(i, i ^ 1) for i in range(plan.scens)]
    edges = partners(plan)

    swap = lambda x: lax.ppermute(x, "scen", flip)
    outer = lambda x: lax.ppermute(x, AXES, edges)
    jump = lambda x, bit: lax.ppermute(x, "scen", [(i, i ^ bit) for i in range(plan.scens)])
    part = lambda f, *a: functools.partial(f, plan, *a)
    half = (2, plan.rank, plan.periods, TILE)
    sums = (plan.blocks, SUB, TILE)
    shares = (plan.groups, plan.blocks, plan.local, SUB, LANE)
    whole = (plan.rows, TILE)
    halves = [(plan.local * (hi - lo), TILE) for lo, hi in plan.parts]
    ranks = range(len(plan.parts))
    bits = [1 << b for b in range(1, plan.scens.bit_length() - 1)]

    def across(x, sent):
        other = None
        for k, bit in enumerate(bits):
            if k:
                x = x + other.astype(f32)
                sent = x.astype(sent.dtype)
            other = jump(sent, bit)
        return x, (jnp.zeros_like(sent) if other is None else other), sent

    packed = [None, None]

    def means_of(sides, short=True, final=False):
        count = len(sides)
        arrays = [(edge[0], inner)[k] for k in sides]
        outs = [(sums, f32)] * count + ([(sums, bf16)] * count if short else [])
        if final:
            outs += [((arrays[0].shape[0] // 2 + plan.blocks * SUB, TILE), f32)]
        got = call(part(means_kernel, short, final), [share, *arrays], outs)
        if final:
            packed[sides[0]] = swap(got[-1])
        return [across(got[k], got[count + k] if short else got[k]) for k in range(count)]

    came = swap(start)
    parts = (2, 2, plan.rank, plan.periods, TILE)
    held, drive_held, drive_sent, control, share, select = call(
        part(prepare_kernel), [],
        [(half, bf16), (half, f32), (half, f32), ((SUB, LANE), jnp.int32), (shares, f32), (shares, f32)],
        far=[cone_list, node_list, probability, start, ore, dual],
        scratch=[
            pltpu.VMEM(parts, bf16),
            pltpu.VMEM(parts, f32),
            *(pltpu.SMEM(x.shape, x.dtype) for x in (cone_list, node_list, probability)),
            pltpu.SemaphoreType.DMA((13,)),
        ],
    )
    n = len(ranks)
    shapes = [*halves, whole]
    got = call(part(start_kernel), [held, came], [(x, f32) for x in shapes] + [(x, bf16) for x in shapes])
    edge, inner = list(got[:n]), got[n]
    halo = [outer(got[n + 1 + c]) for c in ranks]
    halo_n = swap(got[2 * n + 1])
    means = means_of((0, 1))
    drive_came = swap(drive_sent)
    drive = call(part(drive_kernel), [drive_held, drive_came], [(whole, f32)] * 2)
    last = []
    for step in range(ITERS * PG_STEPS):
        closing = step % PG_STEPS == PG_STEPS - 1
        final = step == ITERS * PG_STEPS - 1
        last_round = step >= PG_STEPS
        outs = [(whole, f32), (whole, f32)] + ([] if final else [(whole, bf16)])
        if step % PG_STEPS == 0:
            cone = call(part(cone_kernel), [control, *edge, inner, halo_n, patterns], [(whole, f32)] * 2, after=last)
            arrays = [*edge, inner, *cone, *drive, select, *means[0][:2], *means[1][:2]]
            outs += [(whole, f32)] * 2
            outs += [(whole, f32)] * 2 + [((2, plan.own, TILE), f32)] if last_round else []
            got = call(part(center_kernel, last_round), arrays, outs)
            pull = got[3:5]
            if last_round:
                moved = [*got[5:7], swap(got[7])]
        else:
            arrays = [control, *edge, inner, halo_n, *pull, patterns]
            got = call(part(inside_kernel, final), arrays, outs, after=last)
        base, inner = got[:2]
        last = [base]
        if not final:
            halo_n = swap(got[2])
        if closing:
            means_n = means_of((1,), short=final, final=final)
            last = [means_n[0][2]]
        for c in ranks:
            outs = [(halves[c], f32)] + ([] if final else [(halves[c], bf16)])
            got = call(part(outside_kernel, c), [control, base, halo[c], patterns], outs, after=last)
            edge[c] = got[0]
            last = [got[0]]
            if not final:
                halo[c] = outer(got[1])
            if closing and c == 0:
                means = means_of((0,), final=final) + means_n
                last = [means[0][2]]
    packed_rest = [swap(call(part(pick_kernel), [edge[1]], [((plan.rank * (plan.periods - plan.top), TILE), f32)])[0])] if n > 1 else []
    (fraction,) = call(part(fraction_kernel), [*edge, inner, packed[1], packed[0], *packed_rest], [(start.shape, f32)])
    prices = (plan.rank, plan.top, plan.width)
    (price,) = call(part(price_kernel), [dual, edge[0], inner, *packed, *moved], [(prices, f32)])
    if len(bits) == 1:
        theirs = [(packed[k], jump(means[k][2], 3)) for k in range(2)]
        offsets = tuple(x.shape[0] - plan.blocks * SUB for x in packed)
    else:
        theirs = [(swap(means[k][0]), swap(means[k][1])) for k in range(2)]
        offsets = (0, 0)
    arrays = [price, select, *means[0][:2], *means[1][:2], *theirs[0], *theirs[1]]
    (dual_out,) = call(
        part(finish_kernel, offsets), [dual, *arrays], [(start.shape, f32)], far_out=True,
        scratch=[pltpu.VMEM(prices, f32), pltpu.SemaphoreType.DMA((plan.rank + 1,))],
    )
    return fraction, dual_out


def solution(mesh):
    def body(start, ore, dual, patterns, cone_list, node_list, probability):
        plan = Plan(mesh, start, cone_list, node_list)
        assert plan.tiles == 4 and plan.scens % 2 == 0 and plan.periods % SUB == 0
        return tiled(plan, start, ore, dual, patterns, cone_list, node_list, probability)

    split = P("scen", None, "space")
    in_specs = (split, split, split, P(), P("space", None), P(), P())
    return jax.shard_map(body, mesh=mesh, in_specs=in_specs, out_specs=(split, split), check_vma=False)
```
